128 devices in a mesh: depth: 8 (over y_hi, x), freq: 16 (over y_lo, z, core).
Axes of the slice: x: 4, y: 4 (y_hi: 2, y_lo: 2; y = y_hi * 2 + y_lo), z: 4, core: 2. Of those that a mesh axis runs over, the one named last changes fastest.
Arguments:
- source: bfloat16 [16, 2, 1024, 256], P('freq'), may hold values from -6 to 6
- propagator: bfloat16 [8, 16, 2, 1024, 1024], P('depth', 'freq'), may hold values from -0.125 to 0.125
- transmission: float32 [8, 16, 1024], P('depth', 'freq'), may hold values from 0.5 to 1.5
- upgoing: bfloat16 [8, 16, 2, 1024, 256], P('depth', 'freq'), may hold values from -6 to 6
Outputs:
- gradient: float32 [8, 1024, 2, 1024], P('depth', 'freq')
The draws below stay inside these ranges and needn't reach their ends.
All inputs are finite; a program needn't handle non-finite values.
Results may differ from the reference program's by a relative error of at most 0.013.
Values may be sent and summed in bfloat16 or wider, within the bound.
A program may use at most 64 MiB of HBM per device.

```python
import jax
import jax.numpy as jnp
from jax import lax

NX = 1024
SHOTS = 256
LEVELS = 8
FREQS = 16


def strengthened(values, rng, source, target, shards_of, factor):
    def block_of(axis_at):
        return (jnp.arange(values.shape[axis_at]) // (values.shape[axis_at] // shards_of)).reshape((-1,) + (1,) * (values.ndim - 1 - axis_at))

    first = jax.random.permutation(rng, shards_of)[block_of(target)]
    far = (block_of(target) + shards_of // 2) % shards_of
    return jnp.where((block_of(source) == first) | (block_of(source) == far), factor * values, values)


def level_of(own_key, shape, cuts, least, top_value):
    factor_of = 1.0
    for dim, parts in cuts:
        steps = jax.random.uniform(jax.random.fold_in(jax.random.fold_in(own_key, 6), dim), (parts,), jnp.float32, least / len(cuts), top_value / len(cuts))
        factor_of = factor_of * jnp.repeat(jnp.exp(steps), shape[dim] // parts).reshape((-1,) + (1,) * (len(shape) - 1 - dim))
    return factor_of


def gaussian(stream_key, extent, scale, bound, shards=(), kind=jnp.bfloat16):
    entries = jax.random.normal(stream_key, extent, jnp.float32) * scale
    if len(shards) > 0:
        entries = level_of(stream_key, extent, shards, -0.22, 0.18) * entries
    return jnp.clip(entries, min=-bound, max=bound).astype(kind)


def noise_with(stream_key, shape, scale, reach, shards, heavy, held_as=jnp.bfloat16):
    drawn = scale * jax.random.normal(stream_key, shape, jnp.float32)
    if shards:
        drawn = drawn * level_of(stream_key, shape, shards, -0.22, 0.18)
    return jnp.clip(strengthened(drawn, jax.random.fold_in(stream_key, 3), *heavy), -reach, reach).astype(held_as)


def setup_inputs(seed: int = 0) -> dict:
    splits = jax.random.split(jax.random.key(seed), 5)
    return {
        "source": gaussian(splits[0], (FREQS, 2, NX, SHOTS), 1.0, 6.0, ((0, 16),)),
        "propagator": gaussian(splits[1], (LEVELS, FREQS, 2, NX, NX), (2 * NX) ** -0.5, 0.125, ((0, 8), (1, 16))),
        "transmission": jnp.clip(1.0 + 0.1 * jax.random.normal(splits[2], (LEVELS, FREQS, NX), jnp.float32), 0.5, 1.5),
        "upgoing": noise_with(splits[3], (LEVELS, FREQS, 2, NX, SHOTS), 1.0, 6.0, ((0, 8), (1, 16)), (1, 3, 16, 2.0)),
    }


def advance(panel, weight, factor):
    shots = panel.shape[1] // 2
    real_part = jnp.dot(weight[0], panel, preferred_element_type=jnp.float32)
    imag_part = jnp.dot(weight[1], panel, preferred_element_type=jnp.float32)
    out_real = real_part[:, :shots] - imag_part[:, shots:]
    out_imag = real_part[:, shots:] + imag_part[:, :shots]
    joined = jnp.concatenate([out_real, out_imag], axis=1)
    return (joined * factor[:, None]).astype(jnp.bfloat16)


def correlate(upward, panel):
    up_pair = jnp.concatenate([upward[0], upward[1]], axis=1)
    up_turn = jnp.concatenate([upward[1], -upward[0]], axis=1)
    dims = (((1,), (1,)), ((), ()))
    real_part = lax.dot_general(up_pair, panel, dims, preferred_element_type=jnp.float32)
    imag_part = lax.dot_general(up_turn, panel, dims, preferred_element_type=jnp.float32)
    return jnp.stack([real_part, imag_part], axis=1)


def reference(source, propagator, transmission, upgoing):
    levels = propagator.shape[0]
    freqs = propagator.shape[1]
    width = propagator.shape[3]
    shots = source.shape[3]
    factor = (2.0 * shots * freqs) ** -0.5

    def one_freq(carry, index):
        panel = jnp.concatenate([source[index, 0], source[index, 1]], axis=1)
        outputs = []
        for level in range(levels):
            panel = advance(panel, propagator[level, index], transmission[level, index])
            outputs.append(carry[level] + correlate(upgoing[level, index], panel))
        return jnp.stack(outputs), None

    start = jnp.zeros((levels, width, 2, width), jnp.float32)
    total, _ = lax.scan(one_freq, start, jnp.arange(freqs, dtype=jnp.int32))
    return total * factor
```

```python
import functools

import jax
import jax.numpy as jnp
from jax import lax
from jax.experimental import pallas as pl
from jax.experimental.pallas import tpu as pltpu
from jax.sharding import PartitionSpec as P

MESH = pl.DeviceIdType.MESH
BF16 = jnp.bfloat16
F32 = jnp.float32

CHUNKS = 8
TILE = 256
ORDERS = ((1, 2, 4), (2, 4, 1), (4, 1, 2))
TILE_ORDER = (0, 3, 6, 1, 4, 7, 2, 5)


def order_of(tile):
    return ORDERS[tile // 3]


def chip_at(z, y, relative):
    near = (z, z + 1 - 2 * (z % 2), 3 - z, (z + 2) % 4)[relative % 4]
    return (1 - y if relative >= 4 else y), near


def dot_nt(a, b):
    return lax.dot_general(a, b, (((1,), (1,)), ((), ())), preferred_element_type=F32)


def dot_nn(a, b):
    return lax.dot_general(a, b, (((1,), (0,)), ((), ())), preferred_element_type=F32)


def kernel(
    levels, scale,
    src_hbm, w_hbm, t_hbm, u_hbm, out_ref,
    src_ref, w_ref, t_ref, u_ref, lhs_ref, p_ref, q_ref, acc_ref, s_ref, r1_ref, r2_ref, r3_ref,
    load_sem, uload_sem, usend_sem, urecv_sem, psend_sem, precv_sem, qsend_sem, qrecv_sem, ssend_sem, srecv_sem,
):
    level = lax.axis_index("depth")
    freq = lax.axis_index("freq")
    core = freq % 2
    z = (freq // 2) % 4
    y = freq // 8
    partner = (level, freq + 1 - 2 * core)
    after = (level + 1, freq)
    before = (level - 1, freq)

    def freq_at(relative):
        y_at, z_at = chip_at(z, y, relative)
        return y_at * 8 + z_at * 2 + core

    def block_at(relative):
        y_at, z_at = chip_at(z, y, relative)
        return y_at * 4 + z_at

    shots = p_ref.shape[1]
    width = p_ref.shape[2]
    count = shots // CHUNKS
    half = shots // 2
    rows = out_ref.shape[1]
    tiles = width // TILE
    kept = u_ref.shape[2]

    src_copy = pltpu.make_async_copy(src_hbm, src_ref, load_sem.at[0])
    t_copy = pltpu.make_async_copy(t_hbm, t_ref, load_sem.at[1])
    w_copies = [
        pltpu.make_async_copy(
            w_hbm.at[:, pl.ds(m * TILE, TILE), :], w_ref.at[:, pl.ds(m * TILE, TILE), :], load_sem.at[2 + m]
        )
        for m in range(tiles)
    ]
    u_copies = [
        pltpu.make_async_copy(u_hbm.at[:, block_at(r), core], u_ref.at[0, :, r], uload_sem.at[r]) for r in range(kept)
    ]

    @pl.when(level == 0)
    def _():
        src_copy.start()

    t_copy.start()
    for copy in w_copies:
        copy.start()
    for copy in u_copies:
        copy.start()

    barrier = pltpu.get_barrier_semaphore()
    sides = [partner] + [(level, freq_at(bit)) for bit in (1, 2, 4)]
    for device in sides:
        pl.semaphore_signal(barrier, inc=1, device_id=device, device_id_type=MESH)

    @pl.when(level > 0)
    def _():
        pl.semaphore_signal(barrier, inc=1, device_id=before, device_id_type=MESH)

    @pl.when(level < levels - 1)
    def _():
        pl.semaphore_signal(barrier, inc=1, device_id=after, device_id_type=MESH)

    inner = (level > 0) & (level < levels - 1)

    @pl.when(inner)
    def _():
        pl.semaphore_wait(barrier, len(sides) + 2)

    @pl.when(jnp.logical_not(inner))
    def _():
        pl.semaphore_wait(barrier, len(sides) + 1)

    def u_swap(r):
        return pltpu.make_async_remote_copy(
            u_hbm.at[:, block_at(r), 1 - core], u_ref.at[1, :, r], usend_sem.at[r], urecv_sem.at[r],
            device_id=partner, device_id_type=MESH,
        )

    for r in range(kept):
        u_swap(r).start()

    def make_lhs():
        for copy in u_copies:
            copy.wait()
        for r in range(kept):
            u_swap(r).wait_recv()
        for part in range(2):
            span = pl.ds(part * half, half)
            for slot in range(2):
                real = u_ref[slot, 0, :, :, span].reshape(kept * rows, half)
                imag = u_ref[slot, 1, :, :, span].reshape(kept * rows, half)
                lhs_ref[part, 0, :, pl.ds(slot * 2 * half, half)] = real
                lhs_ref[part, 0, :, pl.ds(slot * 2 * half + half, half)] = imag
                lhs_ref[part, 1, :, pl.ds(slot * 2 * half, half)] = imag
                lhs_ref[part, 1, :, pl.ds(slot * 2 * half + half, half)] = -real

    @pl.when(level == 0)
    def _():
        src_copy.wait()
        for plane in range(2):
            for part in range(2):
                p_ref[plane, pl.ds(part * half, half), :] = src_ref[plane, :, pl.ds(part * half, half)].T

    @pl.when(level > 0)
    def _():
        make_lhs()

    t_copy.wait()
    for copy in w_copies:
        copy.wait()

    def span_of(c):
        return pl.ds(pl.multiple_of(c * count, count), count)

    def onward(c):
        return pltpu.make_async_remote_copy(
            q_ref.at[0, :, span_of(c), :], p_ref.at[:, span_of(c), :], psend_sem.at[c], precv_sem.at[c],
            device_id=after, device_id_type=MESH,
        )

    def across(c):
        return pltpu.make_async_remote_copy(
            q_ref.at[0, :, span_of(c), :], q_ref.at[1, :, span_of(c), :], qsend_sem.at[c], qrecv_sem.at[c],
            device_id=partner, device_id_type=MESH,
        )

    def advance(c):
        span = span_of(c)

        @pl.when(level > 0)
        def _():
            onward(c).wait_recv()

        real = p_ref[0, span, :]
        imag = p_ref[1, span, :]
        plain = jnp.concatenate([real, imag], axis=0)
        turned = jnp.concatenate([-imag, real], axis=0)
        for m in range(tiles):
            cols = pl.ds(m * TILE, TILE)
            total = dot_nt(plain, w_ref[0, cols, :]) + dot_nt(turned, w_ref[1, cols, :])
            total = (total * t_ref[:, cols]).astype(BF16)
            q_ref[0, 0, span, cols] = total[:count]
            q_ref[0, 1, span, cols] = total[count:]

        @pl.when(level < levels - 1)
        def _():
            onward(c).start()

        across(c).start()

    def product(part, plane, cols):
        span = pl.ds(part * half, half)
        rhs = jnp.concatenate([q_ref[slot, p, span, cols] for slot in range(2) for p in range(2)], axis=0)
        return dot_nn(lhs_ref[part, plane], rhs)

    def first(c, carry):
        advance(c)
        return carry

    lax.fori_loop(0, CHUNKS // 2, first, 0)

    @pl.when(level == 0)
    def _():
        make_lhs()

    for c in range(CHUNKS // 2):
        across(c).wait_recv()

    def second(c, carry):
        advance(CHUNKS // 2 + c)
        for plane in range(2):
            cols = pl.ds(pl.multiple_of(c * TILE, TILE), TILE)
            acc_ref[plane, c] = product(0, plane, cols)
        return carry

    lax.fori_loop(0, tiles, second, 0)
    for c in range(CHUNKS // 2, CHUNKS):
        across(c).wait_recv()

    landing = (r1_ref, r2_ref, r3_ref)

    def piece(tile, step, r):
        bit = order_of(tile)[step]
        at = sum(4 >> s for s in range(step))
        index = at + sum((1 << i) for i, b in enumerate(order_of(tile)[step + 1:]) if r & b)
        cols = pl.ds(tile * TILE, TILE)
        return pltpu.make_async_remote_copy(
            s_ref.at[r, :, cols], landing[step].at[r - bit, :, cols],
            ssend_sem.at[tile, index], srecv_sem.at[tile, index],
            device_id=(level, freq_at(bit)), device_id_type=MESH,
        )

    def sets(tile):
        a, b, c = order_of(tile)
        return ((a + b + c, a + b, a + c, a), (b + c, b), (c,))

    def kept_block(tile, r):
        return acc_ref[tile // tiles, tile % tiles, pl.ds(r * rows, rows), :]

    for tile in TILE_ORDER:
        plane, col = tile // tiles, tile % tiles
        cols = pl.ds(tile * TILE, TILE)
        acc_ref[plane, col] += product(1, plane, pl.ds(col * TILE, TILE))
        for r in sets(tile)[0]:
            s_ref[r, :, cols] = kept_block(tile, r).astype(BF16)
            piece(tile, 0, r).start()

    for tile in TILE_ORDER:
        a, b, c = order_of(tile)
        cols = pl.ds(tile * TILE, TILE)
        for r in (b + c, b):
            piece(tile, 0, r + a).wait_recv()
            s_ref[r, :, cols] = (kept_block(tile, r) + r1_ref[r, :, cols].astype(F32)).astype(BF16)
            piece(tile, 1, r).start()

    for tile in TILE_ORDER:
        a, b, c = order_of(tile)
        cols = pl.ds(tile * TILE, TILE)
        piece(tile, 0, c + a).wait_recv()
        piece(tile, 1, c + b).wait_recv()
        s_ref[c, :, cols] = (
            kept_block(tile, c) + r1_ref[c, :, cols].astype(F32) + r2_ref[c, :, cols].astype(F32)
        ).astype(BF16)
        piece(tile, 2, c).start()

    for tile in TILE_ORDER:
        a, b, c = order_of(tile)
        cols = pl.ds(tile * TILE, TILE)
        piece(tile, 0, a).wait_recv()
        piece(tile, 1, b).wait_recv()
        piece(tile, 2, c).wait_recv()
        total = kept_block(tile, 0) + r1_ref[0, :, cols].astype(F32)
        total = total + r2_ref[0, :, cols].astype(F32) + r3_ref[0, :, cols].astype(F32)
        out_ref[tile // tiles, :, pl.ds((tile % tiles) * TILE, TILE)] = total * scale

    for r in range(kept):
        u_swap(r).wait_send()
    for c in range(CHUNKS):
        across(c).wait_send()

        @pl.when(level < levels - 1)
        def _():
            onward(c).wait_send()

    for tile in TILE_ORDER:
        for step, leaving in enumerate(sets(tile)):
            for r in leaving:
                piece(tile, step, r).wait_send()


def shards(source, propagator, transmission, upgoing):
    levels = lax.axis_size("depth")
    freqs = lax.axis_size("freq")
    width = propagator.shape[3]
    shots = source.shape[3]
    rows = width // freqs
    kept = freqs // 2
    tiles = width // TILE
    scale = (2.0 * shots * freqs) ** (-0.5)
    dma = pltpu.SemaphoreType.DMA
    summed = pl.pallas_call(
        functools.partial(kernel, levels, scale),
        out_shape=jax.ShapeDtypeStruct((2, rows, width), F32),
        in_specs=[pl.BlockSpec(memory_space=pl.ANY)] * 4,
        out_specs=pl.BlockSpec(memory_space=pltpu.VMEM),
        scratch_shapes=[
            pltpu.VMEM((2, width, shots), BF16),
            pltpu.VMEM((2, width, width), BF16),
            pltpu.VMEM((1, width), F32),
            pltpu.VMEM((2, 2, kept, rows, shots), BF16),
            pltpu.VMEM((2, 2, kept * rows, 2 * shots), BF16),
            pltpu.VMEM((2, shots, width), BF16),
            pltpu.VMEM((2, 2, shots, width), BF16),
            pltpu.VMEM((2, tiles, kept * rows, TILE), F32),
            pltpu.VMEM((kept, rows, 2 * width), BF16),
            pltpu.VMEM((kept, rows, 2 * width), BF16),
            pltpu.VMEM((kept, rows, 2 * width), BF16),
            pltpu.VMEM((kept, rows, 2 * width), BF16),
            dma((2 + tiles,)),
            dma((kept,)),
            dma((kept,)),
            dma((kept,)),
            dma((CHUNKS,)),
            dma((CHUNKS,)),
            dma((CHUNKS,)),
            dma((CHUNKS,)),
            dma((2 * tiles, 7)),
            dma((2 * tiles, 7)),
        ],
        compiler_params=pltpu.CompilerParams(
            collective_id=0, has_side_effects=True, vmem_limit_bytes=60 * 1024 * 1024
        ),
    )(
        source.reshape(2, width, shots),
        propagator.reshape(2, width, width),
        transmission.reshape(1, width),
        upgoing.reshape(2, kept, 2, rows, shots),
    )
    return jnp.transpose(summed, (1, 0, 2)).reshape(1, rows, 2, width)


def solution(mesh):
    return jax.shard_map(
        shards,
        mesh=mesh,
        in_specs=(
            P("freq", None, None, None),
            P("depth", "freq", None, None, None),
            P("depth", "freq", None),
            P("depth", "freq", None, None, None),
        ),
        out_specs=P("depth", "freq", None, None),
        check_vma=False,
    )
```

```python
import functools

import jax
import jax.numpy as jnp
from jax import lax
from jax.experimental import pallas as pl
from jax.experimental.pallas import tpu as pltpu
from jax.sharding import PartitionSpec as P

MESH = pl.DeviceIdType.MESH
BF16 = jnp.bfloat16
F32 = jnp.float32

CHUNKS = 16
PIECES = 2
TILE = 256
ORDERS = ((1, 2, 4), (2, 4, 1), (4, 1, 2))
TILE_ORDER = (0, 3, 6, 1, 4, 7, 2, 5)


def order_of(tile):
    return ORDERS[tile // 3]


def chip_at(z, y, relative):
    near = (z, z + 1 - 2 * (z % 2), 3 - z, (z + 2) % 4)[relative % 4]
    return (1 - y if relative >= 4 else y), near


def dot_nt(a, b):
    return lax.dot_general(a, b, (((1,), (1,)), ((), ())), preferred_element_type=F32)


def dot_nn(a, b):
    return lax.dot_general(a, b, (((1,), (0,)), ((), ())), preferred_element_type=F32)


def kernel(
    levels, scale,
    src_hbm, w_hbm, t_hbm, u_hbm, out_ref,
    src_ref, w_ref, wt_ref, t_ref, u_ref, p_ref, q_ref, acc_ref, s_ref, r1_ref, r2_ref, r3_ref,
    load_sem, uload_sem, usend_sem, urecv_sem, psend_sem, precv_sem, qsend_sem, qrecv_sem, ssend_sem, srecv_sem,
):
    level = lax.axis_index("depth")
    freq = lax.axis_index("freq")
    core = freq % 2
    z = (freq // 2) % 4
    y = freq // 8
    partner = (level, freq + 1 - 2 * core)
    after = (level + 1, freq)
    before = (level - 1, freq)

    def freq_at(relative):
        y_at, z_at = chip_at(z, y, relative)
        return y_at * 8 + z_at * 2 + core

    def block_at(relative):
        y_at, z_at = chip_at(z, y, relative)
        return y_at * 4 + z_at

    count = p_ref.shape[2] // 2
    deep = p_ref.shape[3]
    width = deep * PIECES
    shots = count * CHUNKS
    half = shots // 2
    halfway = CHUNKS // 2
    kept = u_ref.shape[2]
    rows = u_ref.shape[3]
    tiles = width // TILE

    src_copy = pltpu.make_async_copy(src_hbm, src_ref, load_sem.at[0])
    t_copy = pltpu.make_async_copy(t_hbm, t_ref, load_sem.at[1])
    w_copies = [
        pltpu.make_async_copy(
            w_hbm.at[:, pl.ds(m * TILE, TILE), :], w_ref.at[:, pl.ds(m * TILE, TILE), :], load_sem.at[2 + m]
        )
        for m in range(tiles)
    ]
    u_copies = [
        pltpu.make_async_copy(u_hbm.at[:, block_at(r), core], u_ref.at[0, :, r], uload_sem.at[r]) for r in range(kept)
    ]

    @pl.when(level == 0)
    def _():
        src_copy.start()

    for copy in w_copies:
        copy.start()
    t_copy.start()
    for copy in u_copies:
        copy.start()

    barrier = pltpu.get_barrier_semaphore()
    sides = [partner] + [(level, freq_at(bit)) for bit in (1, 2, 4)]
    for device in sides:
        pl.semaphore_signal(barrier, inc=1, device_id=device, device_id_type=MESH)

    @pl.when(level > 0)
    def _():
        pl.semaphore_signal(barrier, inc=1, device_id=before, device_id_type=MESH)

    @pl.when(level < levels - 1)
    def _():
        pl.semaphore_signal(barrier, inc=1, device_id=after, device_id_type=MESH)

    def turn_source(part):
        for k in range(PIECES):
            for plane in range(2):
                block = src_ref[plane, pl.ds(k * deep, deep), pl.ds(part * half, half)].T
                p_ref[pl.ds(part * halfway, halfway), k, pl.ds(plane * count, count), :] = block.reshape(
                    halfway, count, deep
                )

    @pl.when(level == 0)
    def _():
        src_copy.wait()
        turn_source(0)

    inner = (level > 0) & (level < levels - 1)

    @pl.when(inner)
    def _():
        pl.semaphore_wait(barrier, len(sides) + 2)

    @pl.when(jnp.logical_not(inner))
    def _():
        pl.semaphore_wait(barrier, len(sides) + 1)

    def u_swap(r):
        return pltpu.make_async_remote_copy(
            u_hbm.at[:, block_at(r), 1 - core], u_ref.at[1, :, r], usend_sem.at[r], urecv_sem.at[r],
            device_id=partner, device_id_type=MESH,
        )

    for r in range(kept):
        u_swap(r).start()

    t_copy.wait()
    for m in range(tiles):
        w_copies[m].wait()

        @pl.when(level > 0)
        def _():
            for k in range(PIECES):
                for plane in range(2):
                    block = w_ref[plane, pl.ds(m * TILE, TILE), pl.ds(k * deep, deep)]
                    wt_ref[k, pl.ds(plane * deep, deep), pl.ds(m * TILE, TILE)] = block.T

    def onward(c, k):
        return pltpu.make_async_remote_copy(
            q_ref.at[0, c, k], p_ref.at[c, k], psend_sem.at[c, k], precv_sem.at[c, k],
            device_id=after, device_id_type=MESH,
        )

    def across(c):
        return pltpu.make_async_remote_copy(
            q_ref.at[0, c], q_ref.at[1, c], qsend_sem.at[c], qrecv_sem.at[c],
            device_id=partner, device_id_type=MESH,
        )

    def chunk_lhs(c, k):
        real = p_ref[c, k, pl.ds(0, count), :]
        imag = p_ref[c, k, pl.ds(count, count), :]
        return jnp.concatenate([real, imag], axis=0), jnp.concatenate([-imag, real], axis=0)

    def scaled(total, m):
        return (total * t_ref[:, pl.ds(m * deep, deep)]).astype(BF16)

    def open_chunks(b):
        sides = [[chunk_lhs(2 * b + i, k) for k in range(PIECES)] for i in range(2)]
        plain, turned = (
            jnp.concatenate(
                [jnp.concatenate([sides[i][k][which] for i in range(2)], axis=0) for k in range(PIECES)], axis=1
            )
            for which in range(2)
        )
        for m in range(PIECES):
            cols = pl.ds(m * deep, deep)
            total = scaled(dot_nt(plain, w_ref[0, cols, :]) + dot_nt(turned, w_ref[1, cols, :]), m)
            for i in range(2):
                q_ref[0, 2 * b + i, m] = total[i * 2 * count:(i + 1) * 2 * count]
                onward(2 * b + i, m).start()
        for i in range(2):
            across(2 * b + i).start()

    def advance(c):
        totals = [None] * PIECES
        for k in range(PIECES):
            onward(c, k).wait_recv()
            lhs = jnp.concatenate(chunk_lhs(c, k), axis=1)
            for m in range(PIECES):
                part = dot_nn(lhs, wt_ref[k, :, pl.ds(m * deep, deep)])
                totals[m] = part if k == 0 else totals[m] + part
                if k == PIECES - 1:
                    q_ref[0, c, m] = scaled(totals[m], m)

                    @pl.when(level < levels - 1)
                    def _():
                        onward(c, m).start()

        across(c).start()

    def product(part, plane, col):
        first = part * halfway
        k, cols = col * TILE // deep, pl.ds(pl.multiple_of(col * TILE % deep, TILE), TILE)
        lhs, rhs = [], []
        for slot in range(2):
            real = q_ref[slot, pl.ds(first, halfway), k, pl.ds(0, count), cols].reshape(half, TILE)
            imag = q_ref[slot, pl.ds(first, halfway), k, pl.ds(count, count), cols].reshape(half, TILE)
            u_real, u_imag = (
                u_ref[slot, p, :, :, pl.ds(part * half, half)].reshape(kept * rows, half) for p in range(2)
            )
            lhs += [u_imag, u_real] if plane else [u_real, u_imag]
            rhs += [real, -imag] if plane else [real, imag]
        return dot_nn(jnp.concatenate(lhs, axis=1), jnp.concatenate(rhs, axis=0))

    def first_half(tile):
        acc_ref[tile] = product(0, tile // tiles, tile % tiles)

    def ready(part):
        for c in range(part * halfway, (part + 1) * halfway):
            across(c).wait_recv()

    def swapped():
        for r in range(kept):
            u_copies[r].wait()
            u_swap(r).wait_recv()

    @pl.when(level == 0)
    def _():
        def opening(b, carry):
            open_chunks(b)
            return carry

        lax.fori_loop(0, halfway // 2, opening, 0)
        turn_source(1)
        lax.fori_loop(halfway // 2, halfway, opening, 0)
        swapped()
        ready(0)
        for tile in range(2 * tiles):
            first_half(tile)

    @pl.when(level > 0)
    def _():
        def early(c, carry):
            advance(c)
            return carry

        lax.fori_loop(0, halfway, early, 0)
        swapped()
        ready(0)
        for plane in range(2):
            def late(col, carry):
                advance(halfway + plane * tiles + col)
                acc_ref[plane * tiles + col] = product(0, plane, col)
                return carry

            lax.fori_loop(0, tiles, late, 0)

    ready(1)

    landing = (r1_ref, r2_ref, r3_ref)

    def piece(tile, step, r):
        bit = order_of(tile)[step]
        at = sum(4 >> s for s in range(step))
        index = at + sum((1 << i) for i, b in enumerate(order_of(tile)[step + 1:]) if r & b)
        return pltpu.make_async_remote_copy(
            s_ref.at[tile, r], landing[step].at[tile, r - bit],
            ssend_sem.at[tile, index], srecv_sem.at[tile, index],
            device_id=(level, freq_at(bit)), device_id_type=MESH,
        )

    def own(tile, r):
        return acc_ref[tile, pl.ds(r * rows, rows), :]

    for tile in TILE_ORDER:
        a, b, c = order_of(tile)
        acc_ref[tile] += product(1, tile // tiles, tile % tiles)
        for r in (a + b + c, a + b, a + c):
            s_ref[tile, r] = own(tile, r).astype(BF16)
            piece(tile, 0, r).start()

    for more in (True, False):
        for tile in TILE_ORDER:
            a, b, c = order_of(tile)
            r = b + c if more else b
            piece(tile, 0, r + a).wait_recv()
            s_ref[tile, r] = (own(tile, r) + r1_ref[tile, r].astype(F32)).astype(BF16)
            piece(tile, 1, r).start()

    for tile in TILE_ORDER:
        a, b, c = order_of(tile)
        piece(tile, 0, c + a).wait_recv()
        piece(tile, 1, c + b).wait_recv()
        s_ref[tile, c] = (own(tile, c) + r1_ref[tile, c].astype(F32) + r2_ref[tile, c].astype(F32)).astype(BF16)
        piece(tile, 2, c).start()

    for tile in TILE_ORDER:
        a, b, c = order_of(tile)
        s_ref[tile, a] = own(tile, a).astype(BF16)
        piece(tile, 0, a).start()

    for tile in TILE_ORDER:
        a, b, c = order_of(tile)
        piece(tile, 1, b).wait_recv()
        piece(tile, 2, c).wait_recv()
        piece(tile, 0, a).wait_recv()
        total = own(tile, 0) + r1_ref[tile, 0].astype(F32)
        total = total + r2_ref[tile, 0].astype(F32) + r3_ref[tile, 0].astype(F32)
        out_ref[tile // tiles, :, pl.ds((tile % tiles) * TILE, TILE)] = total * scale

    for r in range(kept):
        u_swap(r).wait_send()
    for c in range(CHUNKS):
        across(c).wait_send()

    @pl.when(level < levels - 1)
    def _():
        for c in range(CHUNKS):
            for k in range(PIECES):
                onward(c, k).wait_send()

    for tile in TILE_ORDER:
        a, b, c = order_of(tile)
        for r in (a + b + c, a + b, a + c, a):
            piece(tile, 0, r).wait_send()
        for r in (b + c, b):
            piece(tile, 1, r).wait_send()
        piece(tile, 2, c).wait_send()


def shards(source, propagator, transmission, upgoing):
    levels = lax.axis_size("depth")
    freqs = lax.axis_size("freq")
    width = propagator.shape[3]
    shots = source.shape[3]
    rows = width // freqs
    kept = freqs // 2
    tiles = width // TILE
    count = shots // CHUNKS
    deep = width // PIECES
    scale = (2.0 * shots * freqs) ** (-0.5)
    dma = pltpu.SemaphoreType.DMA
    summed = pl.pallas_call(
        functools.partial(kernel, levels, scale),
        out_shape=jax.ShapeDtypeStruct((2, rows, width), F32),
        in_specs=[pl.BlockSpec(memory_space=pl.ANY)] * 4,
        out_specs=pl.BlockSpec(memory_space=pltpu.VMEM),
        scratch_shapes=[
            pltpu.VMEM((2, width, shots), BF16),
            pltpu.VMEM((2, width, width), BF16),
            pltpu.VMEM((PIECES, 2 * deep, width), BF16),
            pltpu.VMEM((1, width), F32),
            pltpu.VMEM((2, 2, kept, rows, shots), BF16),
            pltpu.VMEM((CHUNKS, PIECES, 2 * count, deep), BF16),
            pltpu.VMEM((2, CHUNKS, PIECES, 2 * count, deep), BF16),
            pltpu.VMEM((2 * tiles, kept * rows, TILE), F32),
            pltpu.VMEM((2 * tiles, kept, rows, TILE), BF16),
            pltpu.VMEM((2 * tiles, kept, rows, TILE), BF16),
            pltpu.VMEM((2 * tiles, kept, rows, TILE), BF16),
            pltpu.VMEM((2 * tiles, kept, rows, TILE), BF16),
            dma((2 + tiles,)),
            dma((kept,)),
            dma((kept,)),
            dma((kept,)),
            dma((CHUNKS, PIECES)),
            dma((CHUNKS, PIECES)),
            dma((CHUNKS,)),
            dma((CHUNKS,)),
            dma((2 * tiles, 7)),
            dma((2 * tiles, 7)),
        ],
        compiler_params=pltpu.CompilerParams(
            collective_id=0, has_side_effects=True, vmem_limit_bytes=60 * 1024 * 1024
        ),
    )(
        source.reshape(2, width, shots),
        propagator.reshape(2, width, width),
        transmission.reshape(1, width),
        upgoing.reshape(2, kept, 2, rows, shots),
    )
    return jnp.transpose(summed, (1, 0, 2)).reshape(1, rows, 2, width)


def solution(mesh):
    return jax.shard_map(
        shards,
        mesh=mesh,
        in_specs=(
            P("freq", None, None, None),
            P("depth", "freq", None, None, None),
            P("depth", "freq", None),
            P("depth", "freq", None, None, None),
        ),
        out_specs=P("depth", "freq", None, None),
        check_vma=False,
    )
```

```python
import functools

import jax
import jax.numpy as jnp
from jax import lax
from jax.experimental import pallas as pl
from jax.experimental.pallas import tpu as pltpu
from jax.sharding import PartitionSpec as P

MESH = pl.DeviceIdType.MESH
BF16 = jnp.bfloat16
F32 = jnp.float32

CHUNKS = 16
PIECES = 2
TILE = 256
VMEM_LIMIT = 55_000_000
ORDERS = ((1, 4, 2), (2, 4, 1), (4, 1, 2), (1, 4, 2), (2, 4, 1), (4, 2, 1), (1, 2, 4), (2, 1, 4))
TILE_ORDER = (0, 1, 2, 3, 4, 5, 6, 7)


def order_of(tile):
    return ORDERS[tile]


def chip_at(z, y, relative):
    near = (z, z + 1 - 2 * (z % 2), 3 - z, (z + 2) % 4)[relative % 4]
    return (1 - y if relative >= 4 else y), near


def dot_nt(a, b):
    return lax.dot_general(a, b, (((1,), (1,)), ((), ())), preferred_element_type=F32)


def dot_nn(a, b):
    return lax.dot_general(a, b, (((1,), (0,)), ((), ())), preferred_element_type=F32)


def kernel(
    levels, scale,
    src_hbm, w_hbm, t_hbm, u_hbm, out_ref,
    src_ref, w_ref, wt_ref, t_ref, u_ref, p_ref, q_ref, acc_ref, s_ref, r1_ref, r2_ref, r3_ref,
    load_sem, uload_sem, usend_sem, urecv_sem, psend_sem, precv_sem, qsend_sem, qrecv_sem, ssend_sem, srecv_sem,
):
    level = lax.axis_index("depth")
    freq = lax.axis_index("freq")
    core = freq % 2
    z = (freq // 2) % 4
    y = freq // 8
    partner = (level, freq + 1 - 2 * core)
    after = (level + 1, freq)
    before = (level - 1, freq)

    def freq_at(relative):
        y_at, z_at = chip_at(z, y, relative)
        return y_at * 8 + z_at * 2 + core

    def block_at(relative):
        y_at, z_at = chip_at(z, y, relative)
        return y_at * 4 + z_at

    count = p_ref.shape[2] // 2
    deep = p_ref.shape[3]
    width = deep * PIECES
    shots = count * CHUNKS
    half = shots // 2
    halfway = CHUNKS // 2
    kept = u_ref.shape[2]
    rows = u_ref.shape[3]
    tiles = width // TILE

    src_copy = pltpu.make_async_copy(src_hbm, src_ref, load_sem.at[0])
    t_copy = pltpu.make_async_copy(t_hbm, t_ref, load_sem.at[1])
    w_copies = [
        pltpu.make_async_copy(
            w_hbm.at[:, pl.ds(m * TILE, TILE), :], w_ref.at[:, pl.ds(m * TILE, TILE), :], load_sem.at[2 + m]
        )
        for m in range(tiles)
    ]
    u_copies = [
        pltpu.make_async_copy(u_hbm.at[:, block_at(r), core], u_ref.at[0, :, r], uload_sem.at[r]) for r in range(kept)
    ]

    @pl.when(level == 0)
    def _():
        src_copy.start()

    for copy in w_copies:
        copy.start()
    t_copy.start()
    for copy in u_copies:
        copy.start()

    barrier = pltpu.get_barrier_semaphore()
    sides = [partner] + [(level, freq_at(bit)) for bit in (1, 2, 4)]
    for device in sides:
        pl.semaphore_signal(barrier, inc=1, device_id=device, device_id_type=MESH)

    @pl.when(level > 0)
    def _():
        pl.semaphore_signal(barrier, inc=1, device_id=before, device_id_type=MESH)

    @pl.when(level < levels - 1)
    def _():
        pl.semaphore_signal(barrier, inc=1, device_id=after, device_id_type=MESH)

    def turn_source(part):
        for k in range(PIECES):
            for plane in range(2):
                block = src_ref[plane, pl.ds(k * deep, deep), pl.ds(part * half, half)].T
                p_ref[pl.ds(part * halfway, halfway), k, pl.ds(plane * count, count), :] = block.reshape(
                    halfway, count, deep
                )

    def chunk_lhs(c, k):
        real = p_ref[c, k, pl.ds(0, count), :]
        imag = p_ref[c, k, pl.ds(count, count), :]
        return jnp.concatenate([real, imag], axis=0), jnp.concatenate([-imag, real], axis=0)

    def scaled(total, m):
        return (total * t_ref[:, pl.ds(m * deep, deep)]).astype(BF16)

    def open_chunks(b, arrive=lambda m: None):
        sides = [[chunk_lhs(2 * b + i, k) for k in range(PIECES)] for i in range(2)]
        plain, turned = (
            jnp.concatenate(
                [jnp.concatenate([sides[i][k][which] for i in range(2)], axis=0) for k in range(PIECES)], axis=1
            )
            for which in range(2)
        )
        for m in range(PIECES):
            arrive(m)
            cols = pl.ds(m * deep, deep)
            total = scaled(dot_nt(plain, w_ref[0, cols, :]) + dot_nt(turned, w_ref[1, cols, :]), m)
            for i in range(2):
                q_ref[0, 2 * b + i, m] = total[i * 2 * count:(i + 1) * 2 * count]

    @pl.when(level == 0)
    def _():
        src_copy.wait()
        turn_source(0)
        t_copy.wait()

        def arrive(m):
            for i in range(tiles // PIECES):
                w_copies[m * (tiles // PIECES) + i].wait()

        open_chunks(0, arrive)

    inner = (level > 0) & (level < levels - 1)

    @pl.when(inner)
    def _():
        pl.semaphore_wait(barrier, len(sides) + 2)

    @pl.when(jnp.logical_not(inner))
    def _():
        pl.semaphore_wait(barrier, len(sides) + 1)

    def u_swap(r):
        return pltpu.make_async_remote_copy(
            u_hbm.at[:, block_at(r), 1 - core], u_ref.at[1, :, r], usend_sem.at[r], urecv_sem.at[r],
            device_id=partner, device_id_type=MESH,
        )

    for r in range(kept):
        u_swap(r).start()

    @pl.when(level > 0)
    def _():
        t_copy.wait()
        for m in range(tiles):
            w_copies[m].wait()
            for k in range(PIECES):
                for plane in range(2):
                    block = w_ref[plane, pl.ds(m * TILE, TILE), pl.ds(k * deep, deep)]
                    wt_ref[k, pl.ds(plane * deep, deep), pl.ds(m * TILE, TILE)] = block.T

    def onward(c, k):
        return pltpu.make_async_remote_copy(
            q_ref.at[0, c, k], p_ref.at[c, k], psend_sem.at[c, k], precv_sem.at[c, k],
            device_id=after, device_id_type=MESH,
        )

    def across(c):
        return pltpu.make_async_remote_copy(
            q_ref.at[0, c], q_ref.at[1, c], qsend_sem.at[c], qrecv_sem.at[c],
            device_id=partner, device_id_type=MESH,
        )

    def leave_chunks(b):
        for i in range(2):
            for k in range(PIECES):
                onward(2 * b + i, k).start()
        for i in range(2):
            across(2 * b + i).start()

    def advance(c, last):
        totals = [None] * PIECES
        for k in range(PIECES):
            onward(c, k).wait_recv()
            lhs = jnp.concatenate(chunk_lhs(c, k), axis=1)
            for m in range(PIECES):
                part = dot_nn(lhs, wt_ref[k, :, pl.ds(m * deep, deep)])
                totals[m] = part if k == 0 else totals[m] + part
                if k == PIECES - 1:
                    q_ref[0, c, m] = scaled(totals[m], m)
                    if not last:
                        onward(c, m).start()

        across(c).start()

    def product(part, plane, col):
        first = part * halfway
        k, cols = col * TILE // deep, pl.ds(pl.multiple_of(col * TILE % deep, TILE), TILE)
        lhs, rhs = [], []
        for slot in range(2):
            real = q_ref[slot, pl.ds(first, halfway), k, pl.ds(0, count), cols].reshape(half, TILE)
            imag = q_ref[slot, pl.ds(first, halfway), k, pl.ds(count, count), cols].reshape(half, TILE)
            u_real, u_imag = (
                u_ref[slot, p, :, :, pl.ds(part * half, half)].reshape(kept * rows, half) for p in range(2)
            )
            lhs += [u_imag, u_real] if plane else [u_real, u_imag]
            rhs += [real, -imag] if plane else [real, imag]
        return dot_nn(jnp.concatenate(lhs, axis=1), jnp.concatenate(rhs, axis=0))

    def first_half(tile):
        acc_ref[tile] = product(0, tile // tiles, tile % tiles)

    def ready(part):
        for c in range(part * halfway, (part + 1) * halfway):
            across(c).wait_recv()

    def swapped():
        for r in range(kept):
            u_copies[r].wait()
            u_swap(r).wait_recv()

    @pl.when(level == 0)
    def _():
        def opening(b, carry):
            open_chunks(b)
            leave_chunks(b)
            return carry

        leave_chunks(0)
        lax.fori_loop(1, halfway // 2, opening, 0)
        turn_source(1)
        lax.fori_loop(halfway // 2, halfway, opening, 0)
        swapped()

        ready(0)
        ready(1)
        for tile in range(2 * tiles):
            first_half(tile)

    def run(last):
        def early(c, carry):
            advance(c, last)
            return carry

        lax.fori_loop(0, halfway, early, 0)
        swapped()
        ready(0)
        for plane in range(2):
            def late(col, carry):
                advance(halfway + plane * tiles + col, last)
                acc_ref[plane * tiles + col] = product(0, plane, col)
                return carry

            lax.fori_loop(0, tiles, late, 0)
        ready(1)

    @pl.when(inner)
    def _():
        run(False)

    @pl.when(level == levels - 1)
    def _():
        run(True)

    landing = (r1_ref, r2_ref, r3_ref)

    def piece(tile, step, r):
        bit = order_of(tile)[step]
        at = sum(4 >> s for s in range(step))
        index = at + sum((1 << i) for i, b in enumerate(order_of(tile)[step + 1:]) if r & b)
        return pltpu.make_async_remote_copy(
            s_ref.at[tile, r], landing[step].at[tile, r - bit],
            ssend_sem.at[tile, index], srecv_sem.at[tile, index],
            device_id=(level, freq_at(bit)), device_id_type=MESH,
        )

    def own(tile, r):
        return acc_ref[tile, pl.ds(r * rows, rows), :]

    for tile in TILE_ORDER:
        a, b, c = order_of(tile)
        acc_ref[tile] += product(1, tile // tiles, tile % tiles)
        for r in (a + b + c, a + b, a + c):
            s_ref[tile, r] = own(tile, r).astype(BF16)
            piece(tile, 0, r).start()

    for more in (True, False):
        for tile in TILE_ORDER:
            a, b, c = order_of(tile)
            r = b + c if more else b
            piece(tile, 0, r + a).wait_recv()
            s_ref[tile, r] = (own(tile, r) + r1_ref[tile, r].astype(F32)).astype(BF16)
            piece(tile, 1, r).start()

    for tile in TILE_ORDER:
        a, b, c = order_of(tile)
        piece(tile, 0, c + a).wait_recv()
        piece(tile, 1, c + b).wait_recv()
        s_ref[tile, c] = (own(tile, c) + r1_ref[tile, c].astype(F32) + r2_ref[tile, c].astype(F32)).astype(BF16)
        piece(tile, 2, c).start()

    for tile in TILE_ORDER:
        a, b, c = order_of(tile)
        s_ref[tile, a] = own(tile, a).astype(BF16)
        piece(tile, 0, a).start()

    for tile in TILE_ORDER:
        a, b, c = order_of(tile)
        piece(tile, 1, b).wait_recv()
        piece(tile, 2, c).wait_recv()
        piece(tile, 0, a).wait_recv()
        total = own(tile, 0) + r1_ref[tile, 0].astype(F32)
        total = total + r2_ref[tile, 0].astype(F32) + r3_ref[tile, 0].astype(F32)
        total = total * scale
        for i in range(TILE // 128):
            at = (tile % tiles * (TILE // 128) + i) * 2 + tile // tiles
            out_ref[pl.ds(at, rows, stride=width // 64), :] = total[:, i * 128:(i + 1) * 128]

    for r in range(kept):
        u_swap(r).wait_send()
    for c in range(CHUNKS):
        across(c).wait_send()

    @pl.when(level < levels - 1)
    def _():
        for c in range(CHUNKS):
            for k in range(PIECES):
                onward(c, k).wait_send()

    for tile in TILE_ORDER:
        a, b, c = order_of(tile)
        for r in (a + b + c, a + b, a + c, a):
            piece(tile, 0, r).wait_send()
        for r in (b + c, b):
            piece(tile, 1, r).wait_send()
        piece(tile, 2, c).wait_send()


def shards(source, propagator, transmission, upgoing):
    levels = lax.axis_size("depth")
    freqs = lax.axis_size("freq")
    width = propagator.shape[3]
    shots = source.shape[3]
    rows = width // freqs
    kept = freqs // 2
    tiles = width // TILE
    count = shots // CHUNKS
    deep = width // PIECES
    scale = (2.0 * shots * freqs) ** (-0.5)
    dma = pltpu.SemaphoreType.DMA
    summed = pl.pallas_call(
        functools.partial(kernel, levels, scale),
        out_shape=jax.ShapeDtypeStruct((rows * 2 * width // 128, 128), F32),
        in_specs=[pl.BlockSpec(memory_space=pl.ANY)] * 4,
        out_specs=pl.BlockSpec(memory_space=pltpu.VMEM),
        scratch_shapes=[
            pltpu.VMEM((2, width, shots), BF16),
            pltpu.VMEM((2, width, width), BF16),
            pltpu.VMEM((PIECES, 2 * deep, width), BF16),
            pltpu.VMEM((1, width), F32),
            pltpu.VMEM((2, 2, kept, rows, shots), BF16),
            pltpu.VMEM((CHUNKS, PIECES, 2 * count, deep), BF16),
            pltpu.VMEM((2, CHUNKS, PIECES, 2 * count, deep), BF16),
            pltpu.VMEM((2 * tiles, kept * rows, TILE), F32),
            pltpu.VMEM((2 * tiles, kept, rows, TILE), BF16),
            pltpu.VMEM((2 * tiles, kept, rows, TILE), BF16),
            pltpu.VMEM((2 * tiles, kept, rows, TILE), BF16),
            pltpu.VMEM((2 * tiles, kept, rows, TILE), BF16),
            dma((2 + tiles,)),
            dma((kept,)),
            dma((kept,)),
            dma((kept,)),
            dma((CHUNKS, PIECES)),
            dma((CHUNKS, PIECES)),
            dma((CHUNKS,)),
            dma((CHUNKS,)),
            dma((2 * tiles, 7)),
            dma((2 * tiles, 7)),
        ],
        compiler_params=pltpu.CompilerParams(
            collective_id=0, has_side_effects=True, vmem_limit_bytes=VMEM_LIMIT
        ),
    )(
        source.reshape(2, width, shots),
        propagator.reshape(2, width, width),
        transmission.reshape(1, width),
        upgoing.reshape(2, kept, 2, rows, shots),
    )
    summed = summed.reshape(rows, width // 128, 2, 128)
    return jnp.transpose(summed, (0, 2, 1, 3)).reshape(1, rows, 2, width)


def solution(mesh):
    return jax.shard_map(
        shards,
        mesh=mesh,
        in_specs=(
            P("freq", None, None, None),
            P("depth", "freq", None, None, None),
            P("depth", "freq", None),
            P("depth", "freq", None, None, None),
        ),
        out_specs=P("depth", "freq", None, None),
        check_vma=False,
    )
```

```python
import functools

import jax
import jax.numpy as jnp
from jax import lax
from jax.experimental import pallas as pl
from jax.experimental.pallas import tpu as pltpu
from jax.sharding import PartitionSpec as P

MESH = pl.DeviceIdType.MESH
BF16 = jnp.bfloat16
F32 = jnp.float32

CHUNKS = 16
PIECES = 2
TILE = 256
VMEM_LIMIT = 55_000_000
ORDERS = ((1, 4, 2), (2, 4, 1), (4, 1, 2), (1, 4, 2), (2, 4, 1), (4, 2, 1), (1, 2, 4), (2, 1, 4))
TILE_ORDER = (0, 1, 2, 3, 4, 5, 6, 7)


def order_of(tile):
    return ORDERS[tile]


def chip_at(z, y, relative):
    near = (z, z + 1 - 2 * (z % 2), 3 - z, (z + 2) % 4)[relative % 4]
    return (1 - y if relative >= 4 else y), near


def dot_nt(a, b):
    return lax.dot_general(a, b, (((1,), (1,)), ((), ())), preferred_element_type=F32)


def dot_nn(a, b):
    return lax.dot_general(a, b, (((1,), (0,)), ((), ())), preferred_element_type=F32)


def kernel(
    levels, scale,
    src_hbm, w_hbm, t_hbm, u_hbm, out_ref,
    src_ref, w_ref, wt_ref, t_ref, u_ref, p_ref, q_ref, acc_ref, s_ref, r1_ref, r2_ref, r3_ref,
    load_sem, uload_sem, usend_sem, urecv_sem, psend_sem, precv_sem, qsend_sem, qrecv_sem, ssend_sem, srecv_sem,
):
    level = lax.axis_index("depth")
    freq = lax.axis_index("freq")
    core = freq % 2
    z = (freq // 2) % 4
    y = freq // 8
    partner = (level, freq + 1 - 2 * core)
    after = (level + 1, freq)
    before = (level - 1, freq)

    def freq_at(relative):
        y_at, z_at = chip_at(z, y, relative)
        return y_at * 8 + z_at * 2 + core

    def block_at(relative):
        y_at, z_at = chip_at(z, y, relative)
        return y_at * 4 + z_at

    count = p_ref.shape[2] // 2
    deep = p_ref.shape[3]
    width = deep * PIECES
    shots = count * CHUNKS
    half = shots // 2
    halfway = CHUNKS // 2
    kept = u_ref.shape[2]
    rows = u_ref.shape[3]
    tiles = width // TILE

    src_copies = [
        pltpu.make_async_copy(
            src_hbm.at[:, :, pl.ds(part * half, half)], src_ref.at[part], load_sem.at[2 + tiles + part]
        )
        for part in range(2)
    ]
    t_copy = pltpu.make_async_copy(t_hbm, t_ref, load_sem.at[0])
    w_copies = [
        pltpu.make_async_copy(
            w_hbm.at[:, pl.ds(m * TILE, TILE), :], w_ref.at[:, pl.ds(m * TILE, TILE), :], load_sem.at[2 + m]
        )
        for m in range(tiles)
    ]
    u_copies = [
        pltpu.make_async_copy(u_hbm.at[:, block_at(r), core], u_ref.at[0, :, r], uload_sem.at[r]) for r in range(kept)
    ]

    @pl.when(level == 0)
    def _():
        src_copies[0].start()

    for copy in w_copies:
        copy.start()
    t_copy.start()

    barrier = pltpu.get_barrier_semaphore()
    sides = [partner] + [(level, freq_at(bit)) for bit in (1, 2, 4)]
    for device in sides:
        pl.semaphore_signal(barrier, inc=1, device_id=device, device_id_type=MESH)

    @pl.when(level > 0)
    def _():
        pl.semaphore_signal(barrier, inc=1, device_id=before, device_id_type=MESH)

    @pl.when(level < levels - 1)
    def _():
        pl.semaphore_signal(barrier, inc=1, device_id=after, device_id_type=MESH)

    def turn_source(part):
        for k in range(PIECES):
            for plane in range(2):
                block = src_ref[part, plane, pl.ds(k * deep, deep), :].T
                p_ref[pl.ds(part * halfway, halfway), k, pl.ds(plane * count, count), :] = block.reshape(
                    halfway, count, deep
                )

    def chunk_lhs(c, k):
        real = p_ref[c, k, pl.ds(0, count), :]
        imag = p_ref[c, k, pl.ds(count, count), :]
        return jnp.concatenate([real, imag], axis=0), jnp.concatenate([-imag, real], axis=0)

    def scaled(total, m):
        return (total * t_ref[:, pl.ds(m * deep, deep)]).astype(BF16)

    def open_piece(b, m, both):
        cols = pl.ds(m * deep, deep)
        plain, turned = both
        total = scaled(dot_nt(plain, w_ref[0, cols, :]) + dot_nt(turned, w_ref[1, cols, :]), m)
        for i in range(2):
            q_ref[0, 2 * b + i, m] = total[i * 2 * count:(i + 1) * 2 * count]

    def open_lhs(b):
        sides = [[chunk_lhs(2 * b + i, k) for k in range(PIECES)] for i in range(2)]
        return [
            jnp.concatenate(
                [jnp.concatenate([sides[i][k][which] for i in range(2)], axis=0) for k in range(PIECES)], axis=1
            )
            for which in range(2)
        ]

    def arrive(m):
        for i in range(tiles // PIECES):
            w_copies[m * (tiles // PIECES) + i].wait()

    @pl.when(level == 0)
    def _():
        src_copies[0].wait()
        turn_source(0)
        t_copy.wait()
        arrive(0)
        open_piece(0, 0, open_lhs(0))

    inner = (level > 0) & (level < levels - 1)

    @pl.when(inner)
    def _():
        pl.semaphore_wait(barrier, len(sides) + 2)

    @pl.when(jnp.logical_not(inner))
    def _():
        pl.semaphore_wait(barrier, len(sides) + 1)

    def onward(c, k):
        return pltpu.make_async_remote_copy(
            q_ref.at[0, c, k], p_ref.at[c, k], psend_sem.at[c, k], precv_sem.at[c, k],
            device_id=after, device_id_type=MESH,
        )

    def across(c):
        return pltpu.make_async_remote_copy(
            q_ref.at[0, c], q_ref.at[1, c], qsend_sem.at[c], qrecv_sem.at[c],
            device_id=partner, device_id_type=MESH,
        )

    def leave_chunks(b):
        for i in range(2):
            for k in range(PIECES):
                onward(2 * b + i, k).start()
        for i in range(2):
            across(2 * b + i).start()

    @pl.when(level == 0)
    def _():
        onward(0, 0).start()
        for m in range(1, PIECES):
            arrive(m)
            open_piece(0, m, open_lhs(0))
            onward(0, m).start()
        for m in range(PIECES):
            onward(1, m).start()
        for i in range(2):
            across(i).start()
        src_copies[1].start()

    def u_swap(r):
        return pltpu.make_async_remote_copy(
            u_hbm.at[:, block_at(r), 1 - core], u_ref.at[1, :, r], usend_sem.at[r], urecv_sem.at[r],
            device_id=partner, device_id_type=MESH,
        )

    for r in range(kept):
        u_swap(r).start()
        u_copies[r].start()

    @pl.when(level > 0)
    def _():
        t_copy.wait()
        for m in range(tiles):
            w_copies[m].wait()
            for k in range(PIECES):
                for plane in range(2):
                    block = w_ref[plane, pl.ds(m * TILE, TILE), pl.ds(k * deep, deep)]
                    wt_ref[k, pl.ds(plane * deep, deep), pl.ds(m * TILE, TILE)] = block.T

    def advance(c, last):
        totals = [None] * PIECES
        for k in range(PIECES):
            onward(c, k).wait_recv()
            lhs = jnp.concatenate(chunk_lhs(c, k), axis=1)
            for m in range(PIECES):
                part = dot_nn(lhs, wt_ref[k, :, pl.ds(m * deep, deep)])
                totals[m] = part if k == 0 else totals[m] + part
                if k == PIECES - 1:
                    q_ref[0, c, m] = scaled(totals[m], m)
                    if not last:
                        onward(c, m).start()

        across(c).start()

    def product(part, plane, col, slots=(0, 1)):
        first = part * halfway
        k, cols = col * TILE // deep, pl.ds(pl.multiple_of(col * TILE % deep, TILE), TILE)
        lhs, rhs = [], []
        for slot in slots:
            real = q_ref[slot, pl.ds(first, halfway), k, pl.ds(0, count), cols].reshape(half, TILE)
            imag = q_ref[slot, pl.ds(first, halfway), k, pl.ds(count, count), cols].reshape(half, TILE)
            u_real, u_imag = (
                u_ref[slot, p, :, :, pl.ds(part * half, half)].reshape(kept * rows, half) for p in range(2)
            )
            lhs += [u_imag, u_real] if plane else [u_real, u_imag]
            rhs += [real, -imag] if plane else [real, imag]
        return dot_nn(jnp.concatenate(lhs, axis=1), jnp.concatenate(rhs, axis=0))

    def first_half(tile):
        acc_ref[tile] = product(0, tile // tiles, tile % tiles)

    def own_half():
        for tile in range(2 * tiles):
            acc_ref[tile] += product(1, tile // tiles, tile % tiles, (0,))

    def ready(part):
        for c in range(part * halfway, (part + 1) * halfway):
            across(c).wait_recv()

    def swapped():
        for r in range(kept):
            u_copies[r].wait()
            u_swap(r).wait_recv()

    @pl.when(level == 0)
    def _():
        def opening(b, carry):
            both = open_lhs(b)
            for m in range(PIECES):
                open_piece(b, m, both)
            leave_chunks(b)
            return carry

        lax.fori_loop(1, halfway // 2, opening, 0)
        src_copies[1].wait()
        turn_source(1)
        lax.fori_loop(halfway // 2, halfway, opening, 0)
        swapped()

        ready(0)
        ready(1)
        for tile in range(2 * tiles):
            first_half(tile)
        own_half()

    def run(last):
        def early(c, carry):
            advance(c, last)
            return carry

        lax.fori_loop(0, halfway, early, 0)
        swapped()
        ready(0)
        for plane in range(2):
            def late(col, carry):
                advance(halfway + plane * tiles + col, last)
                acc_ref[plane * tiles + col] = product(0, plane, col)
                return carry

            lax.fori_loop(0, tiles, late, 0)
        own_half()
        ready(1)

    @pl.when(inner)
    def _():
        run(False)

    @pl.when(level == levels - 1)
    def _():
        run(True)

    landing = (r1_ref, r2_ref, r3_ref)

    def piece(tile, step, r):
        bit = order_of(tile)[step]
        at = sum(4 >> s for s in range(step))
        index = at + sum((1 << i) for i, b in enumerate(order_of(tile)[step + 1:]) if r & b)
        return pltpu.make_async_remote_copy(
            s_ref.at[tile, r], landing[step].at[tile, r - bit],
            ssend_sem.at[tile, index], srecv_sem.at[tile, index],
            device_id=(level, freq_at(bit)), device_id_type=MESH,
        )

    def own(tile, r):
        return acc_ref[tile, pl.ds(r * rows, rows), :]

    for tile in TILE_ORDER:
        a, b, c = order_of(tile)
        acc_ref[tile] += product(1, tile // tiles, tile % tiles, (1,))
        for r in (a + b + c, a + b, a + c):
            s_ref[tile, r] = own(tile, r).astype(BF16)
            piece(tile, 0, r).start()

    for more in (True, False):
        for tile in TILE_ORDER:
            a, b, c = order_of(tile)
            r = b + c if more else b
            piece(tile, 0, r + a).wait_recv()
            s_ref[tile, r] = (own(tile, r) + r1_ref[tile, r].astype(F32)).astype(BF16)
            piece(tile, 1, r).start()

    for tile in TILE_ORDER:
        a, b, c = order_of(tile)
        piece(tile, 0, c + a).wait_recv()
        piece(tile, 1, c + b).wait_recv()
        s_ref[tile, c] = (own(tile, c) + r1_ref[tile, c].astype(F32) + r2_ref[tile, c].astype(F32)).astype(BF16)
        piece(tile, 2, c).start()

    for tile in TILE_ORDER:
        a, b, c = order_of(tile)
        s_ref[tile, a] = own(tile, a).astype(BF16)
        piece(tile, 0, a).start()

    for tile in TILE_ORDER:
        a, b, c = order_of(tile)
        piece(tile, 1, b).wait_recv()
        piece(tile, 2, c).wait_recv()
        piece(tile, 0, a).wait_recv()
        total = own(tile, 0) + r1_ref[tile, 0].astype(F32)
        total = total + r2_ref[tile, 0].astype(F32) + r3_ref[tile, 0].astype(F32)
        total = total * scale
        for i in range(TILE // 128):
            at = (tile % tiles * (TILE // 128) + i) * 2 + tile // tiles
            out_ref[pl.ds(at, rows, stride=width // 64), :] = total[:, i * 128:(i + 1) * 128]

    for r in range(kept):
        u_swap(r).wait_send()
    for c in range(CHUNKS):
        across(c).wait_send()

    @pl.when(level < levels - 1)
    def _():
        for c in range(CHUNKS):
            for k in range(PIECES):
                onward(c, k).wait_send()

    for tile in TILE_ORDER:
        a, b, c = order_of(tile)
        for r in (a + b + c, a + b, a + c, a):
            piece(tile, 0, r).wait_send()
        for r in (b + c, b):
            piece(tile, 1, r).wait_send()
        piece(tile, 2, c).wait_send()


def shards(source, propagator, transmission, upgoing):
    levels = lax.axis_size("depth")
    freqs = lax.axis_size("freq")
    width = propagator.shape[3]
    shots = source.shape[3]
    rows = width // freqs
    kept = freqs // 2
    tiles = width // TILE
    count = shots // CHUNKS
    deep = width // PIECES
    scale = (2.0 * shots * freqs) ** (-0.5)
    dma = pltpu.SemaphoreType.DMA
    summed = pl.pallas_call(
        functools.partial(kernel, levels, scale),
        out_shape=jax.ShapeDtypeStruct((rows * 2 * width // 128, 128), F32),
        in_specs=[pl.BlockSpec(memory_space=pl.ANY)] * 4,
        out_specs=pl.BlockSpec(memory_space=pltpu.VMEM),
        scratch_shapes=[
            pltpu.VMEM((2, 2, width, shots // 2), BF16),
            pltpu.VMEM((2, width, width), BF16),
            pltpu.VMEM((PIECES, 2 * deep, width), BF16),
            pltpu.VMEM((1, width), F32),
            pltpu.VMEM((2, 2, kept, rows, shots), BF16),
            pltpu.VMEM((CHUNKS, PIECES, 2 * count, deep), BF16),
            pltpu.VMEM((2, CHUNKS, PIECES, 2 * count, deep), BF16),
            pltpu.VMEM((2 * tiles, kept * rows, TILE), F32),
            pltpu.VMEM((2 * tiles, kept, rows, TILE), BF16),
            pltpu.VMEM((2 * tiles, kept, rows, TILE), BF16),
            pltpu.VMEM((2 * tiles, kept, rows, TILE), BF16),
            pltpu.VMEM((2 * tiles, kept, rows, TILE), BF16),
            dma((4 + tiles,)),
            dma((kept,)),
            dma((kept,)),
            dma((kept,)),
            dma((CHUNKS, PIECES)),
            dma((CHUNKS, PIECES)),
            dma((CHUNKS,)),
            dma((CHUNKS,)),
            dma((2 * tiles, 7)),
            dma((2 * tiles, 7)),
        ],
        compiler_params=pltpu.CompilerParams(
            collective_id=0, has_side_effects=True, vmem_limit_bytes=VMEM_LIMIT
        ),
    )(
        source.reshape(2, width, shots),
        propagator.reshape(2, width, width),
        pltpu.with_memory_space_constraint(transmission.reshape(1, width), pltpu.HBM),
        upgoing.reshape(2, kept, 2, rows, shots),
    )
    summed = summed.reshape(rows, width // 128, 2, 128)
    return jnp.transpose(summed, (0, 2, 1, 3)).reshape(1, rows, 2, width)


def solution(mesh):
    return jax.shard_map(
        shards,
        mesh=mesh,
        in_specs=(
            P("freq", None, None, None),
            P("depth", "freq", None, None, None),
            P("depth", "freq", None),
            P("depth", "freq", None, None, None),
        ),
        out_specs=P("depth", "freq", None, None),
        check_vma=False,
    )
```

```python
import functools

import jax
import jax.numpy as jnp
from jax import lax
from jax.experimental import pallas as pl
from jax.experimental.pallas import tpu as pltpu
from jax.sharding import PartitionSpec as P

MESH = pl.DeviceIdType.MESH
BF16 = jnp.bfloat16
F32 = jnp.float32

CHUNKS = 16
PIECES = 2
TILE = 256
VMEM_LIMIT = 55_000_000
ORDERS = ((1, 4, 2), (2, 4, 1), (4, 1, 2), (1, 4, 2), (2, 4, 1), (4, 2, 1), (1, 2, 4), (2, 1, 4))
TILE_ORDER = (0, 1, 2, 3, 4, 5, 6, 7)


def order_of(tile):
    return ORDERS[tile]


def chip_at(z, y, relative):
    near = (z, z + 1 - 2 * (z % 2), 3 - z, (z + 2) % 4)[relative % 4]
    return (1 - y if relative >= 4 else y), near


def dot_nt(a, b):
    return lax.dot_general(a, b, (((1,), (1,)), ((), ())), preferred_element_type=F32)


def dot_nn(a, b):
    return lax.dot_general(a, b, (((1,), (0,)), ((), ())), preferred_element_type=F32)


def kernel(
    levels, scale,
    src_hbm, w_hbm, t_hbm, u_hbm, out_ref,
    src_ref, w_ref, wt_ref, t_ref, u_ref, p_ref, q_ref, acc_ref, s_ref, r1_ref, r2_ref, r3_ref,
    load_sem, uload_sem, usend_sem, urecv_sem, psend_sem, precv_sem, qsend_sem, qrecv_sem, ssend_sem, srecv_sem,
):
    level = lax.axis_index("depth")
    freq = lax.axis_index("freq")
    core = freq % 2
    z = (freq // 2) % 4
    y = freq // 8
    partner = (level, freq + 1 - 2 * core)
    after = (level + 1, freq)
    before = (level - 1, freq)

    def freq_at(relative):
        y_at, z_at = chip_at(z, y, relative)
        return y_at * 8 + z_at * 2 + core

    def block_at(relative):
        y_at, z_at = chip_at(z, y, relative)
        return y_at * 4 + z_at

    count = p_ref.shape[2] // 2
    deep = p_ref.shape[3]
    width = deep * PIECES
    shots = count * CHUNKS
    half = shots // 2
    halfway = CHUNKS // 2
    kept = u_ref.shape[2]
    rows = u_ref.shape[3]
    tiles = width // TILE

    src_copies = [
        pltpu.make_async_copy(
            src_hbm.at[:, :, pl.ds(part * half, half)], src_ref.at[part], load_sem.at[2 + tiles + part]
        )
        for part in range(2)
    ]
    t_copy = pltpu.make_async_copy(t_hbm, t_ref, load_sem.at[0])
    w_copies = [
        pltpu.make_async_copy(
            w_hbm.at[:, pl.ds(m * TILE, TILE), :], w_ref.at[:, pl.ds(m * TILE, TILE), :], load_sem.at[2 + m]
        )
        for m in range(tiles)
    ]
    u_copies = [
        pltpu.make_async_copy(u_hbm.at[:, block_at(r), core], u_ref.at[0, :, r], uload_sem.at[r]) for r in range(kept)
    ]

    t_copy.start()

    @pl.when(level == 0)
    def _():
        src_copies[0].start()

    for copy in w_copies:
        copy.start()

    barrier = pltpu.get_barrier_semaphore()
    sides = [partner] + [(level, freq_at(bit)) for bit in (1, 2, 4)]
    for device in sides:
        pl.semaphore_signal(barrier, inc=1, device_id=device, device_id_type=MESH)

    @pl.when(level > 0)
    def _():
        pl.semaphore_signal(barrier, inc=1, device_id=before, device_id_type=MESH)

    @pl.when(level < levels - 1)
    def _():
        pl.semaphore_signal(barrier, inc=1, device_id=after, device_id_type=MESH)

    def turn_source(part):
        for k in range(PIECES):
            for plane in range(2):
                block = src_ref[part, plane, pl.ds(k * deep, deep), :].T
                p_ref[pl.ds(part * halfway, halfway), k, pl.ds(plane * count, count), :] = block.reshape(
                    halfway, count, deep
                )

    def chunk_lhs(c, k):
        real = p_ref[c, k, pl.ds(0, count), :]
        imag = p_ref[c, k, pl.ds(count, count), :]
        return jnp.concatenate([real, imag], axis=0), jnp.concatenate([-imag, real], axis=0)

    def scaled(total, m):
        return (total * t_ref[:, pl.ds(m * deep, deep)]).astype(BF16)

    def open_piece(b, m, both):
        cols = pl.ds(m * deep, deep)
        plain, turned = both
        total = scaled(dot_nt(plain, w_ref[0, cols, :]) + dot_nt(turned, w_ref[1, cols, :]), m)
        for i in range(2):
            q_ref[0, 2 * b + i, m] = total[i * 2 * count:(i + 1) * 2 * count]

    def open_lhs(b):
        sides = [[chunk_lhs(2 * b + i, k) for k in range(PIECES)] for i in range(2)]
        return [
            jnp.concatenate(
                [jnp.concatenate([sides[i][k][which] for i in range(2)], axis=0) for k in range(PIECES)], axis=1
            )
            for which in range(2)
        ]

    def arrive(m):
        for i in range(tiles // PIECES):
            w_copies[m * (tiles // PIECES) + i].wait()

    @pl.when(level == 0)
    def _():
        src_copies[0].wait()
        turn_source(0)
        t_copy.wait()
        arrive(0)
        open_piece(0, 0, open_lhs(0))

    inner = (level > 0) & (level < levels - 1)

    @pl.when(inner)
    def _():
        pl.semaphore_wait(barrier, len(sides) + 2)

    @pl.when(jnp.logical_not(inner))
    def _():
        pl.semaphore_wait(barrier, len(sides) + 1)

    def onward(c, k):
        return pltpu.make_async_remote_copy(
            q_ref.at[0, c, k], p_ref.at[c, k], psend_sem.at[c, k], precv_sem.at[c, k],
            device_id=after, device_id_type=MESH,
        )

    def across(c):
        return pltpu.make_async_remote_copy(
            q_ref.at[0, c], q_ref.at[1, c], qsend_sem.at[c], qrecv_sem.at[c],
            device_id=partner, device_id_type=MESH,
        )

    def leave_chunks(b):
        for i in range(2):
            for k in range(PIECES):
                onward(2 * b + i, k).start()
        for i in range(2):
            across(2 * b + i).start()

    @pl.when(level == 0)
    def _():
        onward(0, 0).start()
        for m in range(1, PIECES):
            arrive(m)
            open_piece(0, m, open_lhs(0))
            onward(0, m).start()
        for m in range(PIECES):
            onward(1, m).start()
        for i in range(2):
            across(i).start()
        src_copies[1].start()

    def u_swap(r):
        return pltpu.make_async_remote_copy(
            u_hbm.at[:, block_at(r), 1 - core], u_ref.at[1, :, r], usend_sem.at[r], urecv_sem.at[r],
            device_id=partner, device_id_type=MESH,
        )

    for r in range(kept):
        u_swap(r).start()
        u_copies[r].start()

    @pl.when(level > 0)
    def _():
        t_copy.wait()
        for m in range(tiles):
            w_copies[m].wait()
            for k in range(PIECES):
                for plane in range(2):
                    block = w_ref[plane, pl.ds(m * TILE, TILE), pl.ds(k * deep, deep)]
                    wt_ref[k, pl.ds(plane * deep, deep), pl.ds(m * TILE, TILE)] = block.T

    def advance(c, last):
        totals = [None] * PIECES
        for k in range(PIECES):
            onward(c, k).wait_recv()
            lhs = jnp.concatenate(chunk_lhs(c, k), axis=1)
            for m in range(PIECES):
                part = dot_nn(lhs, wt_ref[k, :, pl.ds(m * deep, deep)])
                totals[m] = part if k == 0 else totals[m] + part
                if k == PIECES - 1:
                    q_ref[0, c, m] = scaled(totals[m], m)
                    if not last:
                        onward(c, m).start()

        across(c).start()

    def product(part, plane, col, slots=(0, 1)):
        first = part * halfway
        k, cols = col * TILE // deep, pl.ds(pl.multiple_of(col * TILE % deep, TILE), TILE)
        lhs, rhs = [], []
        for slot in slots:
            real = q_ref[slot, pl.ds(first, halfway), k, pl.ds(0, count), cols].reshape(half, TILE)
            imag = q_ref[slot, pl.ds(first, halfway), k, pl.ds(count, count), cols].reshape(half, TILE)
            u_real, u_imag = (
                u_ref[slot, p, :, :, pl.ds(part * half, half)].reshape(kept * rows, half) for p in range(2)
            )
            lhs += [u_imag, u_real] if plane else [u_real, u_imag]
            rhs += [real, -imag] if plane else [real, imag]
        return dot_nn(jnp.concatenate(lhs, axis=1), jnp.concatenate(rhs, axis=0))

    def first_half(tile):
        acc_ref[tile] = product(0, tile // tiles, tile % tiles)

    def own_half():
        for tile in range(2 * tiles):
            acc_ref[tile] += product(1, tile // tiles, tile % tiles, (0,))

    def ready(part):
        for c in range(part * halfway, (part + 1) * halfway):
            across(c).wait_recv()

    def swapped():
        for r in range(kept):
            u_copies[r].wait()
            u_swap(r).wait_recv()

    @pl.when(level == 0)
    def _():
        def opening(b, carry):
            both = open_lhs(b)
            for m in range(PIECES):
                open_piece(b, m, both)
            leave_chunks(b)
            return carry

        lax.fori_loop(1, halfway // 2, opening, 0)
        src_copies[1].wait()
        turn_source(1)
        lax.fori_loop(halfway // 2, halfway, opening, 0)
        swapped()

        ready(0)
        ready(1)
        for tile in range(2 * tiles):
            first_half(tile)
        own_half()

    def run(last):
        def early(c, carry):
            advance(c, last)
            return carry

        lax.fori_loop(0, halfway, early, 0)
        swapped()
        ready(0)
        for plane in range(2):
            def late(col, carry):
                advance(halfway + plane * tiles + col, last)
                acc_ref[plane * tiles + col] = product(0, plane, col)
                return carry

            lax.fori_loop(0, tiles, late, 0)
        own_half()
        ready(1)

    @pl.when(inner)
    def _():
        run(False)

    @pl.when(level == levels - 1)
    def _():
        run(True)

    landing = (r1_ref, r2_ref, r3_ref)

    def piece(tile, step, r):
        bit = order_of(tile)[step]
        at = sum(4 >> s for s in range(step))
        index = at + sum((1 << i) for i, b in enumerate(order_of(tile)[step + 1:]) if r & b)
        return pltpu.make_async_remote_copy(
            s_ref.at[tile, r], landing[step].at[tile, r - bit],
            ssend_sem.at[tile, index], srecv_sem.at[tile, index],
            device_id=(level, freq_at(bit)), device_id_type=MESH,
        )

    def own(tile, r):
        return acc_ref[tile, pl.ds(r * rows, rows), :]

    for tile in TILE_ORDER:
        a, b, c = order_of(tile)
        acc_ref[tile] += product(1, tile // tiles, tile % tiles, (1,))
        for r in (a + b + c, a + b, a + c):
            s_ref[tile, r] = own(tile, r).astype(BF16)
            piece(tile, 0, r).start()

    for more in (True, False):
        for tile in TILE_ORDER:
            a, b, c = order_of(tile)
            r = b + c if more else b
            piece(tile, 0, r + a).wait_recv()
            s_ref[tile, r] = (own(tile, r) + r1_ref[tile, r].astype(F32)).astype(BF16)
            piece(tile, 1, r).start()

    for tile in TILE_ORDER:
        a, b, c = order_of(tile)
        piece(tile, 0, c + a).wait_recv()
        piece(tile, 1, c + b).wait_recv()
        s_ref[tile, c] = (own(tile, c) + r1_ref[tile, c].astype(F32) + r2_ref[tile, c].astype(F32)).astype(BF16)
        piece(tile, 2, c).start()

    for tile in TILE_ORDER:
        a, b, c = order_of(tile)
        s_ref[tile, a] = own(tile, a).astype(BF16)
        piece(tile, 0, a).start()

    for tile in TILE_ORDER:
        a, b, c = order_of(tile)
        piece(tile, 1, b).wait_recv()
        piece(tile, 2, c).wait_recv()
        piece(tile, 0, a).wait_recv()
        total = own(tile, 0) + r1_ref[tile, 0].astype(F32)
        total = total + r2_ref[tile, 0].astype(F32) + r3_ref[tile, 0].astype(F32)
        total = total * scale
        for i in range(TILE // 128):
            at = (tile % tiles * (TILE // 128) + i) * 2 + tile // tiles
            out_ref[pl.ds(at, rows, stride=width // 64), :] = total[:, i * 128:(i + 1) * 128]

    for r in range(kept):
        u_swap(r).wait_send()
    for c in range(CHUNKS):
        across(c).wait_send()

    @pl.when(level < levels - 1)
    def _():
        for c in range(CHUNKS):
            for k in range(PIECES):
                onward(c, k).wait_send()

    for tile in TILE_ORDER:
        a, b, c = order_of(tile)
        for r in (a + b + c, a + b, a + c, a):
            piece(tile, 0, r).wait_send()
        for r in (b + c, b):
            piece(tile, 1, r).wait_send()
        piece(tile, 2, c).wait_send()


def shards(source, propagator, transmission, upgoing):
    levels = lax.axis_size("depth")
    freqs = lax.axis_size("freq")
    width = propagator.shape[3]
    shots = source.shape[3]
    rows = width // freqs
    kept = freqs // 2
    tiles = width // TILE
    count = shots // CHUNKS
    deep = width // PIECES
    scale = (2.0 * shots * freqs) ** (-0.5)
    dma = pltpu.SemaphoreType.DMA
    summed = pl.pallas_call(
        functools.partial(kernel, levels, scale),
        out_shape=jax.ShapeDtypeStruct((rows * 2 * width // 128, 128), F32),
        in_specs=[pl.BlockSpec(memory_space=pl.ANY)] * 4,
        out_specs=pl.BlockSpec(memory_space=pltpu.VMEM),
        scratch_shapes=[
            pltpu.VMEM((2, 2, width, shots // 2), BF16),
            pltpu.VMEM((2, width, width), BF16),
            pltpu.VMEM((PIECES, 2 * deep, width), BF16),
            pltpu.VMEM((1, width), F32),
            pltpu.VMEM((2, 2, kept, rows, shots), BF16),
            pltpu.VMEM((CHUNKS, PIECES, 2 * count, deep), BF16),
            pltpu.VMEM((2, CHUNKS, PIECES, 2 * count, deep), BF16),
            pltpu.VMEM((2 * tiles, kept * rows, TILE), F32),
            pltpu.VMEM((2 * tiles, kept, rows, TILE), BF16),
            pltpu.VMEM((2 * tiles, kept, rows, TILE), BF16),
            pltpu.VMEM((2 * tiles, kept, rows, TILE), BF16),
            pltpu.VMEM((2 * tiles, kept, rows, TILE), BF16),
            dma((4 + tiles,)),
            dma((kept,)),
            dma((kept,)),
            dma((kept,)),
            dma((CHUNKS, PIECES)),
            dma((CHUNKS, PIECES)),
            dma((CHUNKS,)),
            dma((CHUNKS,)),
            dma((2 * tiles, 7)),
            dma((2 * tiles, 7)),
        ],
        compiler_params=pltpu.CompilerParams(
            collective_id=0, has_side_effects=True, vmem_limit_bytes=VMEM_LIMIT
        ),
    )(
        source.reshape(2, width, shots),
        propagator.reshape(2, width, width),
        pltpu.with_memory_space_constraint(transmission.reshape(1, width), pltpu.HBM),
        upgoing.reshape(2, kept, 2, rows, shots),
    )
    summed = summed.reshape(rows, width // 128, 2, 128)
    return jnp.transpose(summed, (0, 2, 1, 3)).reshape(1, rows, 2, width)


def solution(mesh):
    return jax.shard_map(
        shards,
        mesh=mesh,
        in_specs=(
            P("freq", None, None, None),
            P("depth", "freq", None, None, None),
            P("depth", "freq", None),
            P("depth", "freq", None, None, None),
        ),
        out_specs=P("depth", "freq", None, None),
        check_vma=False,
    )
```
